32 devices in a mesh: dp: 8 (over y, x, core), tensor: 4 (over z).
Axes of the slice: x: 2, y: 2, z: 4, core: 2. Of those that a mesh axis runs over, the one named last changes fastest.
Arguments:
- layer_input: bfloat16 [8192, 1536], P(('dp', 'tensor')), may hold values from -6 to 6
- seg_ids: int32 [8192], P('dp'), may hold values from 0 to 39, as said below
- norm_gain: float32 [2, 1536], replicated, may hold values from 0.5 to 1.5
- in_weight: bfloat16 [2, 1536, 2, 3072], P(None, None, None, 'tensor'), may hold values from -0.15625 to 0.15625
- bc_weight: bfloat16 [2, 1536, 256], replicated, may hold values from -0.15625 to 0.15625
- dt_weight: bfloat16 [2, 1536, 48], P(None, None, 'tensor'), may hold values from -0.15625 to 0.15625
- conv_x: float32 [2, 3072, 4], P(None, 'tensor'), may hold values from -3 to 3
- conv_bc: float32 [2, 256, 4], replicated, may hold values from -3 to 3
- conv_x_bias: float32 [2, 3072], P(None, 'tensor'), may hold values from -3 to 3
- conv_bc_bias: float32 [2, 256], replicated, may hold values from -3 to 3
- dt_bias: float32 [2, 48], P(None, 'tensor'), may hold values from -6.9 to -2.25
- a_log: float32 [2, 48], P(None, 'tensor'), may hold values from 0 to 2.77
- d_skip: float32 [2, 48], P(None, 'tensor'), may hold values from 0.5 to 1.5
- gate_gain: float32 [2, 3072], P(None, 'tensor'), may hold values from 0.5 to 1.5
- out_weight: bfloat16 [2, 1536, 3072], P(None, None, 'tensor'), may hold values from -0.109375 to 0.109375
- cotangent: bfloat16 [8192, 1536], P(('dp', 'tensor')), may hold values from -6 to 6
Outputs:
- activations: bfloat16 [8192, 1536], P(('dp', 'tensor'))
- input_grad: bfloat16 [8192, 1536], P(('dp', 'tensor'))
- norm_gain_grad: float32 [2, 1536], P(None, ('dp', 'tensor'))
- in_weight_grad: float32 [2, 1536, 2, 3072], P(None, 'dp', None, 'tensor')
- bc_weight_grad: float32 [2, 1536, 256], P(None, ('dp', 'tensor'))
- dt_weight_grad: float32 [2, 1536, 48], P(None, 'dp', 'tensor')
- conv_x_grad: float32 [2, 3072, 4], P(None, 'tensor')
- conv_bc_grad: float32 [2, 256, 4], P(None, ('dp', 'tensor'))
- conv_x_bias_grad: float32 [2, 3072], P(None, 'tensor')
- conv_bc_bias_grad: float32 [2, 256], P(None, ('dp', 'tensor'))
- dt_bias_grad: float32 [2, 48], P(None, 'tensor')
- a_log_grad: float32 [2, 48], P(None, 'tensor')
- d_skip_grad: float32 [2, 48], P(None, 'tensor')
- gate_gain_grad: float32 [2, 3072], P(None, 'tensor')
- out_weight_grad: float32 [2, 1536, 3072], P(None, 'dp', 'tensor')
The draws below stay inside these ranges and needn't reach their ends.
Inputs may be any that keep to these rules, and one draw needn't show every extreme that they name: `seg_ids`: ids never fall along the tokens; each sequence lies within the 1024 tokens of one index of dp, which holds ids that no other index holds; index i of dp holds ids from 5 i upward and below 5 (i + 1); the first token has id 0 and the last token the largest id; a sequence has at most 1024 tokens, and in every draw some index of dp holds one of exactly 1024.
All inputs are finite; a program needn't handle non-finite values.
Results may differ from the reference program's by a relative error of at most 0.019.
Values may be sent and summed in bfloat16 or wider, within the bound.
No kernel may reach another device: no remote copies, remote signals or barrier semaphores. Data moves between devices by JAX's collectives and lax.ppermute only.
A program may use at most 320 MiB of HBM per device.

```python
from functools import partial
import jax
import jax.numpy as jnp
from jax import lax

D = 1536
HEADS = 48
STATE = 128
CONV = 4
SPAN = 256
LAYERS = 2
TOK_DEV = 1024
INNER = 3072
MAX_LEN = 1024
TOKENS = 8192
N_DP = 8


def draw_seg_ids(key, part):
    shortest = max(MAX_LEN // 4, 1)
    slots = TOK_DEV // shortest + 1
    lengths = jax.random.randint(jax.random.fold_in(key, 11), (N_DP, slots), shortest, MAX_LEN + 1)
    chosen = jax.random.randint(jax.random.fold_in(key, 12), (), 0, N_DP)
    device_rows = jnp.arange(N_DP)
    first_len = jnp.where(device_rows == chosen, MAX_LEN, lengths[:, 0])
    lengths = lengths.at[:, 0].set(first_len)
    bounds = jnp.cumsum(lengths, axis=1)
    positions = jnp.arange(TOK_DEV)
    local_ids = jnp.sum((bounds[:, None, :] <= positions[None, :, None]).astype(jnp.int32), axis=2)
    last_local = local_ids[:, TOK_DEV - 1:]
    from_top = slots - 1 - (last_local - local_ids)
    numbered = jnp.where((device_rows == 0)[:, None], local_ids, from_top)
    global_ids = numbered + device_rows[:, None] * slots
    return global_ids.reshape(-1).astype(jnp.int32)


def shard_levels(key, shape, split, low, high):
    def one(axis_at, parts):
        draws = jax.random.uniform(jax.random.fold_in(jax.random.fold_in(key, 6), axis_at), (parts,), jnp.float32, low / len(split), high / len(split))
        return jnp.repeat(jnp.exp(draws), shape[axis_at] // parts).reshape((-1,) + (1,) * (len(shape) - axis_at - 1))

    factor_of = one(*split[0])
    for cut in split[1:]:
        factor_of = factor_of * one(*cut)
    return factor_of


def centred(stream_key, shape, scale, most, split=(), held_as=jnp.bfloat16):
    entries = jax.random.normal(stream_key, shape, jnp.float32) * scale
    if len(split) > 0:
        entries = shard_levels(stream_key, shape, split, -0.22, 0.18) * entries
    return jnp.clip(entries, min=-most, max=most).astype(held_as)


def setup_inputs(seed: int = 0) -> dict:
    splits = jax.random.split(jax.random.key(seed), 17)
    layer_input = centred(splits[0], (TOKENS, D), 1.0, 6.0, ((0, 32),))
    seg_ids = draw_seg_ids(jax.random.fold_in(splits[16], 71), 0)
    norm_gain = jnp.clip(1.0 + 0.1 * jax.random.normal(splits[2], (LAYERS, D), jnp.float32), 0.5, 1.5)
    in_weight = centred(splits[3], (LAYERS, D, 2, INNER), D ** -0.5, 0.15625, ((3, 4),))
    bc_weight = centred(splits[4], (LAYERS, D, 2 * STATE), D ** -0.5, 0.15625)
    dt_weight = centred(splits[5], (LAYERS, D, HEADS), D ** -0.5, 0.15625, ((2, 4),))
    conv_x = centred(splits[6], (LAYERS, INNER, CONV), CONV ** -0.5, 3.0, ((1, 4),), jnp.float32)
    conv_bc = centred(splits[7], (LAYERS, 2 * STATE, CONV), CONV ** -0.5, 3.0, (), jnp.float32)
    conv_x_bias = centred(splits[8], (LAYERS, INNER), 0.5, 3.0, ((1, 4),), jnp.float32)
    conv_bc_bias = centred(splits[9], (LAYERS, 2 * STATE), 0.5, 3.0, (), jnp.float32)
    dt_bias = jnp.clip(-6.9 + 4.65 * jax.random.uniform(splits[10], (LAYERS, HEADS), jnp.float32) ** shard_levels(splits[10], (LAYERS, HEADS), ((1, 4),), -0.2, 0.2), -6.9, -2.25)
    a_log = jnp.clip(2.77 * jax.random.uniform(splits[11], (LAYERS, HEADS), jnp.float32) ** shard_levels(splits[11], (LAYERS, HEADS), ((1, 4),), -0.2, 0.2), 0.0, 2.77)
    d_skip = jnp.clip(0.5 + 1.0 * jax.random.uniform(splits[12], (LAYERS, HEADS), jnp.float32) ** shard_levels(splits[12], (LAYERS, HEADS), ((1, 4),), -0.2, 0.2), 0.5, 1.5)
    gate_gain = jnp.clip(1.0 + 0.1 * jax.random.normal(splits[13], (LAYERS, INNER), jnp.float32), 0.5, 1.5)
    out_weight = centred(splits[14], (LAYERS, D, INNER), INNER ** -0.5, 0.109375, ((2, 4),))
    cotangent = centred(splits[15], (TOKENS, D), 1.0, 6.0, ((0, 32),))
    return dict(layer_input=layer_input, seg_ids=seg_ids, norm_gain=norm_gain, in_weight=in_weight, bc_weight=bc_weight, dt_weight=dt_weight, conv_x=conv_x, conv_bc=conv_bc, conv_x_bias=conv_x_bias, conv_bc_bias=conv_bc_bias, dt_bias=dt_bias, a_log=a_log, d_skip=d_skip, gate_gain=gate_gain, out_weight=out_weight, cotangent=cotangent)


EPS = 1e-05
HIGH = lax.Precision.HIGHEST

def rms_scale(row_block, gain_row):
    return row_block * lax.rsqrt(lax.optimization_barrier(jnp.mean(row_block * row_block, axis=1, keepdims=True)) + EPS) * gain_row

def causal_conv(inputs, weight, bias_row, seg_ids):
    tap_count = weight.shape[1]
    summed = inputs * weight[:, tap_count - 1] + bias_row
    for offset in range(1, tap_count):
        shifted = jnp.pad(inputs, ((offset, 0), (0, 0)))[:inputs.shape[0]]
        earlier = jnp.pad(seg_ids, (offset, 0), constant_values=-1)[:seg_ids.shape[0]]
        summed = summed + jnp.where((earlier == seg_ids)[:, None], shifted, 0.0) * weight[:, tap_count - 1 - offset]
    return summed

def span_scan(values, step_size, decay_rate, b_rows, c_rows, seg_ids, skip_gain):
    row_count, head_count, head_dim = values.shape
    blocks = row_count // SPAN
    log_step = -step_size * decay_rate
    cumulative = jnp.swapaxes(jnp.cumsum(log_step.reshape(blocks, SPAN, head_count), axis=1), 1, 2)
    seg_block = seg_ids.reshape(blocks, SPAN)
    b_block = b_rows.reshape(blocks, SPAN, -1)
    c_block = c_rows.reshape(blocks, SPAN, -1)
    weighted = (values * step_size[:, :, None]).reshape(blocks, SPAN, head_count, head_dim)
    positions = jnp.arange(SPAN)
    allowed = (seg_block[:, :, None] == seg_block[:, None, :]) & (positions[:, None] >= positions[None, :])
    spread = cumulative[:, :, :, None] - cumulative[:, :, None, :]
    decay_mask = jnp.where(allowed[:, None], jnp.exp(jnp.minimum(spread, 0.0)), 0.0)
    scores = jnp.einsum('btn,bsn->bts', c_block, b_block, precision=HIGH)
    inner_part = jnp.einsum('bhts,bshp->bthp', decay_mask * scores[:, None], weighted, precision=HIGH)
    last_seg = seg_block[:, SPAN - 1]
    to_end = jnp.exp(cumulative[:, :, SPAN - 1:] - cumulative) * (seg_block == last_seg[:, None]).astype(jnp.float32)[:, None, :]
    local_state = jnp.einsum('bhs,bshp,bsn->bhpn', to_end, weighted, b_block, precision=HIGH)
    prior_seg = jnp.concatenate([jnp.full((1,), -1, jnp.int32), last_seg[:-1].astype(jnp.int32)])
    factors = jnp.exp(cumulative[:, :, SPAN - 1]) * (last_seg == prior_seg).astype(jnp.float32)[:, None]

    def advance(carry_state, block_item):
        return (carry_state * block_item[1][:, None, None] + block_item[0], carry_state)
    start_state = jnp.zeros(local_state.shape[1:], jnp.float32)
    final_state, entering = lax.scan(advance, start_state, (local_state, factors))
    carried = jnp.einsum('btn,bhpn->bthp', c_block, entering, precision=HIGH)
    reach_gain = jnp.exp(jnp.swapaxes(cumulative, 1, 2)) * (seg_block == prior_seg[:, None]).astype(jnp.float32)[:, :, None]
    result = inner_part + carried * reach_gain[:, :, :, None] + values.reshape(blocks, SPAN, head_count, head_dim) * skip_gain[:, None]
    return result.reshape(row_count, head_count, head_dim)

def mixer(seg_ids, conv_in_x, conv_in_bc, conv_x, conv_bc, conv_x_bias, conv_bc_bias, dt_raw, dt_bias, a_log, d_skip):
    act_x = jax.nn.silu(causal_conv(conv_in_x, conv_x, conv_x_bias, seg_ids))
    act_bc = jax.nn.silu(causal_conv(conv_in_bc, conv_bc, conv_bc_bias, seg_ids))
    state_count = act_bc.shape[1] // 2
    step_size = jax.nn.softplus(dt_raw + dt_bias)
    row_count, head_count = step_size.shape
    values = act_x.reshape(row_count, head_count, act_x.shape[1] // head_count)
    scan_out = span_scan(values, step_size, jnp.exp(a_log), act_bc[:, :state_count], act_bc[:, state_count:], seg_ids, d_skip)
    return scan_out.reshape(row_count, act_x.shape[1])

def reference(layer_input, seg_ids, norm_gain, in_weight, bc_weight, dt_weight, conv_x, conv_bc, conv_x_bias, conv_bc_bias, dt_bias, a_log, d_skip, gate_gain, out_weight, cotangent):

    def one_shard(grads, shard_data):
        rows_in, shard_segs, cot_rows = shard_data
        grads = list(grads)
        stream = rows_in.astype(jnp.float32)
        stored = []
        for layer_no in range(LAYERS):
            normed = rms_scale(stream, norm_gain[layer_no]).astype(jnp.bfloat16)
            zx_weight = in_weight[layer_no].reshape(D, 2 * INNER)
            zx_rows = jnp.dot(normed, zx_weight, preferred_element_type=jnp.float32)
            gate_rows = zx_rows[:, :INNER]
            conv_in_x = zx_rows[:, INNER:]
            conv_in_bc = jnp.dot(normed, bc_weight[layer_no], preferred_element_type=jnp.float32)
            dt_raw = jnp.dot(normed, dt_weight[layer_no], preferred_element_type=jnp.float32)
            scan_out, pull_back = jax.vjp(partial(mixer, shard_segs), conv_in_x, conv_in_bc, conv_x[layer_no], conv_bc[layer_no], conv_x_bias[layer_no], conv_bc_bias[layer_no], dt_raw, dt_bias[layer_no], a_log[layer_no], d_skip[layer_no])
            gated_rows = scan_out * jax.nn.silu(gate_rows)
            inv_rms = lax.rsqrt(lax.optimization_barrier(jnp.mean(gated_rows * gated_rows, axis=1)) + EPS)
            scaled = (gated_rows * inv_rms[:, None] * gate_gain[layer_no]).astype(jnp.bfloat16)
            stored.append((stream, normed, gate_rows, scan_out, pull_back, gated_rows, inv_rms, scaled))
            stream = stream + jnp.einsum('ti,di->td', scaled, out_weight[layer_no], preferred_element_type=jnp.float32)
        activations = stream.astype(jnp.bfloat16)
        grad_stream = cot_rows.astype(jnp.float32)
        for layer_no in reversed(range(LAYERS)):
            stream_in, normed, gate_rows, scan_out, pull_back, gated_rows, inv_rms, scaled = stored[layer_no]
            grad_rows = grad_stream.astype(jnp.bfloat16)
            out_grad = jnp.einsum('td,ti->di', grad_rows, scaled, preferred_element_type=jnp.float32)
            grad_scaled = jnp.dot(grad_rows, out_weight[layer_no], preferred_element_type=jnp.float32)
            gain_grad = lax.optimization_barrier(jnp.sum(grad_scaled * gated_rows * inv_rms[:, None], axis=0))
            weighted_grad = grad_scaled * gate_gain[layer_no]
            cross_sum = lax.optimization_barrier(jnp.sum(weighted_grad * gated_rows, axis=1))
            grad_gated = inv_rms[:, None] * weighted_grad - gated_rows * (inv_rms ** 3 * cross_sum / INNER)[:, None]
            gate_sigmoid = jax.nn.sigmoid(gate_rows)
            grad_mixed = grad_gated * gate_rows * gate_sigmoid
            grad_gate = grad_gated * scan_out * gate_sigmoid * (1.0 + gate_rows * (1.0 - gate_sigmoid))
            grad_ux, grad_ubc, grad_convx, grad_convbc, grad_biasx, grad_biasbc, grad_dt, grad_dtbias, grad_alog, grad_skip = pull_back(grad_mixed)
            zx_grad = jnp.concatenate([grad_gate, grad_ux], axis=1).astype(jnp.bfloat16)
            dt_rounded = grad_dt.astype(jnp.bfloat16)
            bc_rounded = grad_ubc.astype(jnp.bfloat16)
            in_grad = jnp.einsum('td,tk->dk', normed, zx_grad, preferred_element_type=jnp.float32).reshape(D, 2, INNER)
            dtw_grad = jnp.einsum('td,th->dh', normed, dt_rounded, preferred_element_type=jnp.float32)
            bcw_grad = jnp.einsum('td,tk->dk', normed, bc_rounded, preferred_element_type=jnp.float32)
            grad_normed = jnp.einsum('tk,dk->td', zx_grad, in_weight[layer_no].reshape(D, 2 * INNER), preferred_element_type=jnp.float32)
            grad_normed = grad_normed + jnp.einsum('th,dh->td', dt_rounded, dt_weight[layer_no], preferred_element_type=jnp.float32)
            grad_normed = grad_normed + jnp.einsum('tk,dk->td', bc_rounded, bc_weight[layer_no], preferred_element_type=jnp.float32)
            unused, norm_pull = jax.vjp(rms_scale, stream_in, norm_gain[layer_no])
            grad_in, grad_gain = norm_pull(grad_normed)
            grad_stream = grad_stream + grad_in
            layer_grads = (grad_gain, in_grad, bcw_grad, dtw_grad, grad_convx, grad_convbc, grad_biasx, grad_biasbc, grad_dtbias, grad_alog, grad_skip, gain_grad, out_grad)
            for member, grad_value in enumerate(layer_grads):
                grads[member] = grads[member].at[layer_no].add(grad_value)
        return (tuple(grads), (activations, grad_stream.astype(jnp.bfloat16)))
    shapes_list = (norm_gain.shape, in_weight.shape, bc_weight.shape, dt_weight.shape, conv_x.shape, conv_bc.shape, conv_x_bias.shape, conv_bc_bias.shape, dt_bias.shape, a_log.shape, d_skip.shape, gate_gain.shape, out_weight.shape)
    zeros_init = tuple((jnp.zeros(shape_item, jnp.float32) for shape_item in shapes_list))
    shards = (layer_input.reshape(N_DP, TOK_DEV, D), seg_ids.reshape(N_DP, TOK_DEV), cotangent.reshape(N_DP, TOK_DEV, D))
    grads, outputs = lax.scan(one_shard, zeros_init, shards)
    norm_gain_grad, in_weight_grad, bc_weight_grad, dt_weight_grad, conv_x_grad, conv_bc_grad, conv_x_bias_grad, conv_bc_bias_grad, dt_bias_grad, a_log_grad, d_skip_grad, gate_gain_grad, out_weight_grad = grads
    return (outputs[0].reshape(TOKENS, D), outputs[1].reshape(TOKENS, D), norm_gain_grad, in_weight_grad, bc_weight_grad, dt_weight_grad, conv_x_grad, conv_bc_grad, conv_x_bias_grad, conv_bc_bias_grad, dt_bias_grad, a_log_grad, d_skip_grad, gate_gain_grad, out_weight_grad)
```

```python
from functools import partial

import jax
import jax.numpy as jnp
from jax import lax
from jax.experimental import pallas as pl
from jax.experimental.pallas import tpu as pltpu
from jax.sharding import PartitionSpec as P

SPAN = 256
LANES = 128
HALO = 8
EPS = 1e-05
F32 = jnp.float32
BF16 = jnp.bfloat16
HIGH = lax.Precision.HIGHEST

TAP_OK = 0
REACH_OK = 3
END_OK = 4
SEG = 5
INV_RMS = 6
COEF = 7
NEXT_OK = 8


def dot(a, b, dims=((1,), (0,)), precision=None):
    return lax.dot_general(
        a, b, (dims, ((), ())), precision=precision, preferred_element_type=F32
    )


def spread_heads(table, first, head_dim, lane_is_low):
    return jnp.where(lane_is_low, table[:, first : first + 1], table[:, first + 1 : first + 2])


def all_heads(table, head_count, lane_is_low):
    return jnp.concatenate(
        [spread_heads(table, h, 64, lane_is_low) for h in range(0, head_count, 2)], axis=1
    )


def conv_terms(cat_ref, cols, cw_ref, width):
    pre = cat_ref[pl.ds(HALO, SPAN), :] * cw_ref[3:4, :] + cw_ref[4:5, :]
    for k in range(1, 4):
        pre = pre + (
            cat_ref[pl.ds(HALO - k, SPAN), :]
            * cols[:, TAP_OK + k - 1 : TAP_OK + k]
            * cw_ref[3 - k : 4 - k, :]
        )
    return pre


def sigmoid(x):
    return 1.0 / (1.0 + jnp.exp(-x))


def softplus(x):
    return jnp.maximum(x, 0.0) + jnp.log1p(jnp.exp(-jnp.abs(x)))


def span_tables(dt_rows, hv_ref, cols, seg_row):
    dt = softplus(dt_rows + hv_ref[0:1, :])
    row = lax.broadcasted_iota(jnp.int32, (SPAN, SPAN), 0)
    col = lax.broadcasted_iota(jnp.int32, (SPAN, SPAN), 1)
    lower = (row >= col).astype(F32)
    cum = dot(lower, -dt * hv_ref[1:2, :], precision=HIGH)
    allowed = lower * (cols[:, SEG : SEG + 1] == seg_row).astype(F32)
    return dt, cum, allowed, lower


def forward_kernel(
    seg_ref, cols_ref, nrm_ref, wall_ref, wout_ref, cw_ref, hv_ref, ch_ref,
    part_ref, zx_ref, so_ref, sin_ref, ssq_ref,
    state_ref, cat_ref, act_ref, wte_ref,
    *, inner, states, heads,
):
    block = pl.program_id(0)
    width = inner + 2 * states

    @pl.when(block == 0)
    def _():
        state_ref[...] = jnp.zeros_like(state_ref)
        cat_ref[pl.ds(0, HALO), :] = jnp.zeros((HALO, width), F32)

    @pl.when(block > 0)
    def _():
        cat_ref[pl.ds(0, HALO), :] = cat_ref[pl.ds(SPAN, HALO), :]

    zx_ref[...] = dot(nrm_ref[...], wall_ref[...])
    cat_ref[pl.ds(HALO, SPAN), :] = zx_ref[:, inner : inner + width]
    cols = cols_ref[...]
    pre = conv_terms(cat_ref, cols, cw_ref, width)
    act_ref[...] = pre * sigmoid(pre)
    dt, cum, allowed, _ = span_tables(
        zx_ref[:, inner + width :], hv_ref, cols, seg_ref[...]
    )
    cum_t = cum.T
    b_rows = act_ref[:, inner : inner + states].astype(BF16)
    c_rows = act_ref[:, inner + states :].astype(BF16)
    scores = dot(c_rows, b_rows, ((1,), (1,))) * allowed
    last = cum[SPAN - 1 : SPAN, :]
    to_end = jnp.exp(last - cum) * cols[:, END_OK : END_OK + 1]
    reach = jnp.exp(cum) * cols[:, REACH_OK : REACH_OK + 1]
    lane_low = lax.broadcasted_iota(jnp.int32, (SPAN, LANES), 1) < 64
    state = state_ref[...]
    sin_ref[0] = state
    inter = dot(c_rows, state.astype(BF16))
    ssq = jnp.zeros((SPAN, 1), F32)
    for h in range(0, heads, 2):
        lanes = slice(h * 64, h * 64 + 128)
        x = act_ref[:, lanes]
        w = x * spread_heads(dt, h, 64, lane_low)
        wb = w.astype(BF16)
        wte_ref[:, lanes] = (w * spread_heads(to_end, h, 64, lane_low)).astype(BF16)
        parts = []
        for j in (h, h + 1):
            decay = jnp.exp(jnp.minimum(cum[:, j : j + 1] - cum_t[j : j + 1, :], 0.0))
            parts.append(dot((decay * scores).astype(BF16), wb))
        out = (
            jnp.where(lane_low, parts[0], parts[1])
            + inter[:, lanes] * spread_heads(reach, h, 64, lane_low)
            + x * ch_ref[0:1, lanes]
        )
        so_ref[:, lanes] = out
        gate = zx_ref[:, lanes]
        gated = out * gate * sigmoid(gate)
        ssq = ssq + jnp.sum(gated * gated, axis=1, keepdims=True)
        act_ref[:, lanes] = gated * ch_ref[1:2, lanes]
    ssq_ref[...] = ssq
    factor = jnp.exp(last) * cols[SPAN - 1 : SPAN, REACH_OK : REACH_OK + 1]
    factor_lanes = all_heads(factor, heads, lane_low[0:1])
    state_ref[...] = state * factor_lanes + dot(b_rows, wte_ref[...], ((0,), (0,)))
    part_ref[...] = dot(
        act_ref[:, :inner].astype(BF16), wout_ref[...], ((1,), (1,))
    ).astype(BF16)


def backward_kernel(
    seg_ref, cols_ref, nrm_ref, gr_ref, zx_ref, halo_ref, so_ref, sin_ref, wall_ref, wout_ref,
    cw_ref, hv_ref, ch_ref, ones_ref,
    pn_ref, zxg_ref, sc_ref, cwg_ref, chg_ref, hvg_ref, ngg_ref,
    dstate_ref, cat_ref, pre_ref, act_ref, dcat_ref, g_ref, wb_ref, wte_ref,
    *, inner, states, heads, blocks,
):
    step = pl.program_id(0)
    block = blocks - 1 - step
    width = inner + 2 * states

    @pl.when(step == 0)
    def _():
        dstate_ref[...] = jnp.zeros_like(dstate_ref)
        dcat_ref[pl.ds(SPAN, HALO), :] = jnp.zeros((HALO, width), F32)
        cwg_ref[...] = jnp.zeros_like(cwg_ref)
        chg_ref[...] = jnp.zeros_like(chg_ref)
        hvg_ref[...] = jnp.zeros_like(hvg_ref)
        ngg_ref[...] = jnp.zeros_like(ngg_ref)

    @pl.when(step > 0)
    def _():
        dcat_ref[pl.ds(SPAN, HALO), :] = dcat_ref[pl.ds(0, HALO), :]

    cols = cols_ref[...]
    cat_ref[pl.ds(0, HALO), :] = halo_ref[:, inner : inner + width]
    cat_ref[pl.ds(HALO, SPAN), :] = zx_ref[:, inner : inner + width]
    pre = conv_terms(cat_ref, cols, cw_ref, width)
    pre_ref[...] = pre
    act_ref[...] = pre * sigmoid(pre)
    dt_rows = zx_ref[:, inner + width :]
    dt, cum, allowed, lower = span_tables(dt_rows, hv_ref, cols, seg_ref[...])
    cum_t = cum.T
    last = cum[SPAN - 1 : SPAN, :]
    to_end = jnp.exp(last - cum) * cols[:, END_OK : END_OK + 1]
    reach = jnp.exp(cum) * cols[:, REACH_OK : REACH_OK + 1]
    lane_low = lax.broadcasted_iota(jnp.int32, (SPAN, LANES), 1) < 64
    b_rows = act_ref[:, inner : inner + states].astype(BF16)
    c_rows = act_ref[:, inner + states :].astype(BF16)
    scores = dot(c_rows, b_rows, ((1,), (1,))) * allowed
    state = sin_ref[0]
    state_b = state.astype(BF16)
    dstate = dstate_ref[...]
    dstate_b = dstate.astype(BF16)
    inv_rms = cols[:, INV_RMS : INV_RMS + 1]
    coef = cols[:, COEF : COEF + 1]

    grad_scaled = dot(gr_ref[...], wout_ref[...])
    for h in range(0, heads, 2):
        lanes = slice(h * 64, h * 64 + 128)
        gate = zx_ref[:, lanes]
        sig = sigmoid(gate)
        silu = gate * sig
        out = so_ref[:, lanes]
        gated = out * silu
        normed_gated = gated * inv_rms
        gs = grad_scaled[:, lanes]
        gain = ch_ref[1:2, lanes]
        chg_ref[1:2, lanes] += jnp.sum(gs * normed_gated, axis=0, keepdims=True)
        sc_ref[:, lanes] = (normed_gated * gain).astype(BF16)
        grad_gated = gs * gain * inv_rms - gated * coef
        g = grad_gated * silu
        g_ref[:, lanes] = g
        zxg_ref[:, lanes] = (
            grad_gated * out * sig * (1.0 + gate * (1.0 - sig))
        ).astype(BF16)
        x = act_ref[:, lanes]
        chg_ref[0:1, lanes] += jnp.sum(g * x, axis=0, keepdims=True)
        w = x * spread_heads(dt, h, 64, lane_low)
        wb_ref[:, lanes] = w.astype(BF16)
        wte_ref[:, lanes] = (w * spread_heads(to_end, h, 64, lane_low)).astype(BF16)

    g_t = g_ref[...].T.astype(BF16)
    w_t = wb_ref[...].astype(F32).T.astype(BF16)
    dscores = jnp.zeros((SPAN, SPAN), F32)
    dw_parts = []
    for h in range(heads):
        rows = slice(h * 64, h * 64 + 64)
        gh_t = g_t[rows, :]
        decay = jnp.exp(jnp.minimum(cum[:, h : h + 1] - cum_t[h : h + 1, :], 0.0))
        mixed = (decay * scores).astype(BF16)
        pair = slice((h // 2) * 128, (h // 2) * 128 + 128)
        gh = jnp.where(lane_low == (h % 2 == 0), g_ref[:, pair], 0.0).astype(BF16)
        dmixed = dot(gh, w_t[pair, :])
        dscores = dscores + dmixed * decay
        dw_parts.append(dot(gh_t, mixed))
    dw = jnp.concatenate(dw_parts, axis=0).T
    dscores = (dscores * allowed).astype(BF16)
    from_end = dot(b_rows, dstate_b)
    reach_lanes = all_heads(reach, heads, lane_low)
    end_lanes = all_heads(to_end, heads, lane_low)
    dt_lanes = all_heads(dt, heads, lane_low)
    g = g_ref[...]
    x = act_ref[:, :inner]
    dr = (g * reach_lanes).astype(BF16)
    dc = dot(dr, state_b, ((1,), (1,))) + dot(dscores, b_rows)
    db = dot(wte_ref[...], dstate_b, ((1,), (1,))) + dot(dscores, c_rows, ((0,), (0,)))
    factor = jnp.exp(last) * cols[SPAN - 1 : SPAN, REACH_OK : REACH_OK + 1]
    factor_lanes = all_heads(factor, heads, lane_low[0:1])
    dlast_lanes = (
        jnp.sum(dstate * state, axis=0, keepdims=True) * factor_lanes
        + jnp.sum(wte_ref[...].astype(F32) * from_end, axis=0, keepdims=True)
    )
    dstate_ref[...] = dstate * factor_lanes + dot(c_rows, dr, ((0,), (0,)))
    skip = ch_ref[0:1, :]
    ones = ones_ref[...]
    inter = dot(c_rows, state_b)
    dcum = dot(
        g.astype(BF16).astype(F32) * (so_ref[...] - x * skip - inter * reach_lanes)
        + dr.astype(F32) * inter
        - wb_ref[...].astype(F32) * dw
        - wte_ref[...].astype(F32) * from_end,
        ones,
        precision=HIGH,
    )
    dw = dw + from_end * end_lanes
    ddt = dot(dw * x, ones, precision=HIGH)
    dlast = dot(jnp.broadcast_to(dlast_lanes, (8, inner)), ones, precision=HIGH)[0:1]
    dlog = dot(lower, dcum, ((0,), (0,)), precision=HIGH) + dlast
    rate = hv_ref[1:2, :]
    ddt = ddt - rate * dlog
    ddt_raw = ddt * sigmoid(dt_rows + hv_ref[0:1, :])
    hvg_ref[0:1, :] += jnp.sum(ddt_raw, axis=0, keepdims=True)
    hvg_ref[1:2, :] += jnp.sum(-dt * dlog, axis=0, keepdims=True)
    zxg_ref[:, inner + width :] = ddt_raw.astype(BF16)

    pre = pre_ref[...]
    sig = sigmoid(pre)
    slope = sig * (1.0 + pre * (1.0 - sig))
    dcat_ref[pl.ds(0, SPAN), pl.ds(0, inner)] = (g * skip + dw * dt_lanes) * slope[:, :inner]
    dcat_ref[pl.ds(0, SPAN), pl.ds(inner, states)] = db * slope[:, inner : inner + states]
    dcat_ref[pl.ds(0, SPAN), pl.ds(inner + states, states)] = dc * slope[:, inner + states :]
    dpre = dcat_ref[pl.ds(0, SPAN), :]
    cwg_ref[4:5, :] += jnp.sum(dpre, axis=0, keepdims=True)
    cwg_ref[3:4, :] += jnp.sum(dpre * cat_ref[pl.ds(HALO, SPAN), :], axis=0, keepdims=True)
    du = dpre * cw_ref[3:4, :]
    for k in range(1, 4):
        cwg_ref[3 - k : 4 - k, :] += jnp.sum(
            dpre * (cat_ref[pl.ds(HALO - k, SPAN), :] * cols[:, TAP_OK + k - 1 : TAP_OK + k]),
            axis=0,
            keepdims=True,
        )
        du = du + (
            dcat_ref[pl.ds(k, SPAN), :]
            * cols[:, NEXT_OK + k - 1 : NEXT_OK + k]
            * cw_ref[3 - k : 4 - k, :]
        )
    zxg_ref[:, inner : inner + width] = du.astype(BF16)
    grad_normed = dot(zxg_ref[...], wall_ref[...], ((1,), (1,)))
    pn_ref[...] = grad_normed.astype(BF16)
    ngg_ref[0:1, :] += jnp.sum(grad_normed * nrm_ref[...].astype(F32), axis=0, keepdims=True)


def whole_spec(shape):
    return pl.BlockSpec(shape, lambda i: (0,) * len(shape), pipeline_mode=pl.Buffered(1))


def forward_layer(seg_row, cols, normed, wall, wout, cw, hv, ch, interpret=False):
    rows, model = normed.shape
    inner = ch.shape[1]
    states = (cw.shape[1] - inner) // 2
    heads = inner // 64
    blocks = rows // SPAN
    total = wall.shape[1]
    width = cw.shape[1]
    kernel = partial(forward_kernel, inner=inner, states=states, heads=heads)
    row_spec = lambda n: pl.BlockSpec((SPAN, n), lambda i: (i, 0))
    return pl.pallas_call(
        kernel,
        name="layer_forward",
        grid=(blocks,),
        in_specs=[
            pl.BlockSpec((1, SPAN), lambda i: (0, i)),
            row_spec(LANES),
            row_spec(model),
            whole_spec(wall.shape),
            whole_spec(wout.shape),
            whole_spec(cw.shape),
            whole_spec(hv.shape),
            whole_spec(ch.shape),
        ],
        out_specs=[
            row_spec(model),
            row_spec(total),
            row_spec(inner),
            pl.BlockSpec((1, states, inner), lambda i: (i, 0, 0)),
            row_spec(1),
        ],
        out_shape=[
            jax.ShapeDtypeStruct((rows, model), BF16),
            jax.ShapeDtypeStruct((rows, total), F32),
            jax.ShapeDtypeStruct((rows, inner), F32),
            jax.ShapeDtypeStruct((blocks, states, inner), F32),
            jax.ShapeDtypeStruct((rows, 1), F32),
        ],
        scratch_shapes=[
            pltpu.VMEM((states, inner), F32),
            pltpu.VMEM((SPAN + HALO, width), F32),
            pltpu.VMEM((SPAN, width), F32),
            pltpu.VMEM((SPAN, inner), BF16),
        ],
        compiler_params=pltpu.CompilerParams(
            dimension_semantics=("arbitrary",), vmem_limit_bytes=56 * 2**20
        ),
        interpret=interpret,
    )(seg_row, cols, normed, wall, wout, cw, hv, ch)


def backward_layer(
    seg_row, cols, normed, grad_rows, zx, scan_out, states_in, wall, wout, cw, hv, ch, ones,
    interpret=False,
):
    rows, model = grad_rows.shape
    inner = ch.shape[1]
    states = (cw.shape[1] - inner) // 2
    heads = inner // 64
    blocks = rows // SPAN
    total = wall.shape[1]
    width = cw.shape[1]
    kernel = partial(
        backward_kernel, inner=inner, states=states, heads=heads, blocks=blocks
    )
    row_spec = lambda n: pl.BlockSpec((SPAN, n), lambda i: (blocks - 1 - i, 0))
    keep = lambda shape: pl.BlockSpec(shape, lambda i: (0,) * len(shape))
    per = SPAN // HALO
    return pl.pallas_call(
        kernel,
        name="layer_backward",
        grid=(blocks,),
        in_specs=[
            pl.BlockSpec((1, SPAN), lambda i: (0, blocks - 1 - i)),
            row_spec(LANES),
            row_spec(model),
            row_spec(model),
            row_spec(total),
            pl.BlockSpec(
                (HALO, total), lambda i: (jnp.maximum((blocks - 1 - i) * per - 1, 0), 0)
            ),
            row_spec(inner),
            pl.BlockSpec((1, states, inner), lambda i: (blocks - 1 - i, 0, 0)),
            whole_spec(wall.shape),
            whole_spec(wout.shape),
            whole_spec(cw.shape),
            whole_spec(hv.shape),
            whole_spec(ch.shape),
            whole_spec(ones.shape),
        ],
        out_specs=[
            row_spec(model),
            row_spec(total),
            row_spec(inner),
            keep((8, width)),
            keep((8, inner)),
            keep((8, LANES)),
            keep((8, model)),
        ],
        out_shape=[
            jax.ShapeDtypeStruct((rows, model), BF16),
            jax.ShapeDtypeStruct((rows, total), BF16),
            jax.ShapeDtypeStruct((rows, inner), BF16),
            jax.ShapeDtypeStruct((8, width), F32),
            jax.ShapeDtypeStruct((8, inner), F32),
            jax.ShapeDtypeStruct((8, LANES), F32),
            jax.ShapeDtypeStruct((8, model), F32),
        ],
        scratch_shapes=[
            pltpu.VMEM((states, inner), F32),
            pltpu.VMEM((SPAN + HALO, width), F32),
            pltpu.VMEM((SPAN, width), F32),
            pltpu.VMEM((SPAN, width), F32),
            pltpu.VMEM((SPAN + HALO, width), F32),
            pltpu.VMEM((SPAN, inner), F32),
            pltpu.VMEM((SPAN, inner), BF16),
            pltpu.VMEM((SPAN, inner), BF16),
        ],
        compiler_params=pltpu.CompilerParams(
            dimension_semantics=("arbitrary",), vmem_limit_bytes=60 * 2**20
        ),
        interpret=interpret,
    )(
        seg_row, cols, normed, grad_rows, zx, zx, scan_out, states_in, wall, wout, cw, hv, ch,
        ones,
    )


def others(x, axis):
    size = lax.axis_size(axis)
    return [
        lax.ppermute(x, axis, [(i, (i + s) % size) for i in range(size)])
        for s in range(1, size)
    ]


def small_gather(x, axis):
    size = lax.axis_size(axis)
    parts = [x] + others(x, axis)
    ring = jnp.concatenate(parts[::-1] + parts[:0:-1], axis=0)
    start = (size - 1 - lax.axis_index(axis)) * x.shape[0]
    return lax.dynamic_slice_in_dim(ring, start, size * x.shape[0], 0)


def small_sum(x, axis):
    total = x
    for part in others(x, axis):
        total = total + part
    return total


def doubling_sum(x, axis):
    size = lax.axis_size(axis)
    if size & (size - 1):
        return lax.psum(x, axis)
    reach = 1
    while reach < size:
        x = x + lax.ppermute(x, axis, [(i, i ^ reach) for i in range(size)])
        reach *= 2
    return x


def token_table(seg_ids):
    rows = seg_ids.shape[0]
    seg_block = seg_ids.reshape(rows // SPAN, SPAN)
    last_seg = seg_block[:, SPAN - 1]
    prior_seg = jnp.concatenate([jnp.full((1,), -1, jnp.int32), last_seg[:-1]])
    columns = [None] * 11
    for k in range(1, 4):
        earlier = jnp.pad(seg_ids, (k, 0), constant_values=-1)[:rows]
        later = jnp.pad(seg_ids, (0, k), constant_values=-1)[k:]
        columns[TAP_OK + k - 1] = earlier == seg_ids
        columns[NEXT_OK + k - 1] = later == seg_ids
    columns[REACH_OK] = (seg_block == prior_seg[:, None]).reshape(-1)
    columns[END_OK] = (seg_block == last_seg[:, None]).reshape(-1)
    columns[SEG] = seg_ids
    columns[INV_RMS] = jnp.zeros_like(seg_ids)
    columns[COEF] = jnp.zeros_like(seg_ids)
    table = jnp.stack([column.astype(F32) for column in columns], axis=1)
    return jnp.pad(table, ((0, 0), (0, LANES - len(columns))))


def with_columns(table, inv_rms, coef):
    lane = lax.broadcasted_iota(jnp.int32, table.shape, 1)
    table = jnp.where(lane == INV_RMS, inv_rms[:, None], table)
    return jnp.where(lane == COEF, coef[:, None], table)


def rows_of(parts, count, width):
    stacked = jnp.concatenate([part.reshape(-1, width) for part in parts], axis=0)
    return jnp.pad(stacked, ((0, count - stacked.shape[0]), (0, 0)))


def on_device(
    layer_input, seg_ids, norm_gain, in_weight, bc_weight, dt_weight, conv_x, conv_bc,
    conv_x_bias, conv_bc_bias, dt_bias, a_log, d_skip, gate_gain, out_weight, cotangent,
    interpret=False,
):
    layers = norm_gain.shape[0]
    share = layer_input.shape[0]
    model = in_weight.shape[1]
    inner = in_weight.shape[3]
    heads = dt_weight.shape[2]
    head_dim = inner // heads
    width = inner + bc_weight.shape[2]
    tensor_size = lax.axis_size("tensor")
    inner_all = inner * tensor_size
    own = lax.axis_index("tensor") * share
    dp_size = lax.axis_size("dp")
    place = lax.axis_index("dp") * tensor_size + lax.axis_index("tensor")

    def mine(x):
        return lax.dynamic_slice_in_dim(x, own, share, 0)

    def gather(x):
        return lax.all_gather(x, "tensor", axis=0, tiled=True)

    def scatter(x):
        return lax.psum_scatter(x, "tensor", scatter_dimension=0, tiled=True).astype(F32)

    table = token_table(seg_ids)
    seg_row = seg_ids.astype(F32)[None, :]
    ones = (
        lax.broadcasted_iota(jnp.int32, (inner, LANES), 0) // head_dim
        == lax.broadcasted_iota(jnp.int32, (inner, LANES), 1)
    ).astype(F32)
    wall, wout, cw, hv, ch = [], [], [], [], []
    for l in range(layers):
        wall.append(
            jnp.concatenate(
                [
                    in_weight[l].reshape(model, 2 * inner),
                    bc_weight[l],
                    jnp.pad(dt_weight[l], ((0, 0), (0, LANES - heads))),
                ],
                axis=1,
            )
        )
        wout.append(out_weight[l])
        taps = jnp.concatenate([conv_x[l], conv_bc[l]], axis=0).T
        bias = jnp.concatenate([conv_x_bias[l], conv_bc_bias[l]])[None]
        cw.append(jnp.pad(jnp.concatenate([taps, bias], axis=0), ((0, 3), (0, 0))))
        hv.append(
            jnp.pad(jnp.stack([dt_bias[l], jnp.exp(a_log[l])]), ((0, 6), (0, LANES - heads)))
        )
        ch.append(
            jnp.pad(jnp.stack([jnp.repeat(d_skip[l], head_dim), gate_gain[l]]), ((0, 6), (0, 0)))
        )

    def normalize(rows, gain):
        return rows * lax.rsqrt(jnp.mean(rows * rows, axis=1, keepdims=True) + EPS) * gain

    stream = layer_input.astype(F32)
    stored = []
    for l in range(layers):
        normed = gather(normalize(stream, norm_gain[l]).astype(BF16))
        part, zx, scan_out, states_in, square = forward_layer(
            seg_row, table, normed, wall[l], wout[l], cw[l], hv[l], ch[l], interpret
        )
        inv_rms = lax.rsqrt(small_sum(square[:, 0], "tensor") / inner_all + EPS)
        raw = scatter(part)
        stored.append((stream, normed, zx, scan_out, states_in, inv_rms, raw))
        stream = stream + raw * mine(inv_rms)[:, None]
    activations = stream.astype(BF16)

    grad_stream = cotangent.astype(F32)
    grads = [None] * layers
    for l in reversed(range(layers)):
        stream_in, normed, zx, scan_out, states_in, inv_rms, raw = stored[l]
        grad_own = grad_stream.astype(BF16)
        grad_rows = gather(grad_own)
        cross = jnp.sum(grad_own.astype(F32) * raw, axis=1)
        inv_own = mine(inv_rms)
        coef = small_gather(inv_own * inv_own * inv_own * cross / inner_all, "tensor")
        partial_normed, zx_grad, scaled, cw_grad, ch_grad, hv_grad, ng_grad = backward_layer(
            seg_row, with_columns(table, inv_rms, coef), normed, grad_rows, zx, scan_out,
            states_in, wall[l], wout[l], cw[l], hv[l], ch[l], ones, interpret,
        )
        grad_normed = scatter(partial_normed)
        out_grad = jnp.einsum(
            "td,ti->di", grad_rows, scaled, preferred_element_type=F32
        ).astype(BF16)
        in_grad = jnp.einsum(
            "td,tk->dk", normed, zx_grad, preferred_element_type=F32
        ).astype(BF16)
        out_grad, in_grad = (
            lax.psum_scatter(g, "dp", scatter_dimension=0, tiled=True)
            for g in (out_grad, in_grad)
        )
        small = jnp.concatenate(
            [
                cw_grad[:5, :inner].reshape(-1),
                ch_grad[:2].reshape(-1),
                hv_grad[:2, :heads].reshape(-1),
                cw_grad[:5, inner:].reshape(-1),
                (ng_grad[0] / norm_gain[l]),
            ]
        )
        grads[l] = (out_grad, in_grad, small)
        inv = lax.rsqrt(jnp.mean(stream_in * stream_in, axis=1, keepdims=True) + EPS)
        weighted = grad_normed * norm_gain[l]
        inner_product = jnp.mean(weighted * stream_in, axis=1, keepdims=True)
        grad_stream = grad_stream + inv * weighted - stream_in * (inv * inv * inv * inner_product)
    input_grad = grad_stream.astype(BF16)

    def stack(pick):
        return jnp.stack([pick(grads[l]) for l in range(layers)])

    small = stack(lambda g: g[2])
    size = small.shape[1]
    padded = -(-size // LANES) * LANES
    small = doubling_sum(
        jnp.pad(small, ((0, 0), (0, padded - size))).reshape(-1, LANES), "dp"
    ).reshape(layers, padded)
    edges = [5 * inner, 2 * inner, 2 * heads, 5 * (width - inner), model]
    starts = [sum(edges[:i]) for i in range(len(edges))]
    conv_part, channel_part, head_part = (
        small[:, starts[i] : starts[i] + edges[i]] for i in range(3)
    )
    shared = small_sum(small[:, starts[3] : size], "tensor")
    conv_part = conv_part.reshape(layers, 5, inner)
    channel_part = channel_part.reshape(layers, 2, inner)
    head_part = head_part.reshape(layers, 2, heads)
    bc_part = shared[:, : edges[3]].reshape(layers, 5, width - inner)
    bc_share = (width - inner) // (dp_size * tensor_size)
    bc_part = lax.dynamic_slice_in_dim(bc_part, place * bc_share, bc_share, 2)
    model_share = model // (dp_size * tensor_size)
    norm_gain_grad = lax.dynamic_slice_in_dim(
        shared[:, edges[3] :], place * model_share, model_share, 1
    )
    in_part = stack(lambda g: g[1])
    in_weight_grad = (
        in_part[:, :, : 2 * inner].astype(F32).reshape(layers, model // dp_size, 2, inner)
    )
    bc_rows = in_part[:, :, 2 * inner : inner + width]
    bc_weight_grad = lax.psum_scatter(bc_rows, "tensor", scatter_dimension=1, tiled=True)
    return (
        activations,
        input_grad,
        norm_gain_grad,
        in_weight_grad,
        bc_weight_grad.astype(F32),
        in_part[:, :, inner + width : inner + width + heads].astype(F32),
        conv_part[:, :4].transpose(0, 2, 1),
        bc_part[:, :4].transpose(0, 2, 1),
        conv_part[:, 4],
        bc_part[:, 4],
        head_part[:, 0],
        head_part[:, 1] * jnp.exp(a_log),
        channel_part[:, 0].reshape(layers, heads, head_dim).sum(axis=2),
        channel_part[:, 1],
        stack(lambda g: g[0]).astype(F32),
    )


def solution(mesh):
    tokens = P(("dp", "tensor"), None)
    heads_last = P(None, "tensor")
    placed = (
        tokens,
        P("dp"),
        P(),
        P(None, None, None, "tensor"),
        P(),
        P(None, None, "tensor"),
        P(None, "tensor", None),
        P(),
        heads_last,
        P(),
        heads_last,
        heads_last,
        heads_last,
        heads_last,
        P(None, None, "tensor"),
        tokens,
    )
    return jax.shard_map(
        on_device,
        mesh=mesh,
        in_specs=placed,
        out_specs=(
            tokens,
            tokens,
            P(None, ("dp", "tensor")),
            P(None, "dp", None, "tensor"),
            P(None, ("dp", "tensor"), None),
            P(None, "dp", "tensor"),
            P(None, "tensor", None),
            P(None, ("dp", "tensor"), None),
            heads_last,
            P(None, ("dp", "tensor")),
            heads_last,
            heads_last,
            heads_last,
            heads_last,
            P(None, "dp", "tensor"),
        ),
        check_vma=False,
    )
```
